512 devices in a mesh: ctx: 64 (over z_lo, x, core), dp: 8 (over y, z_hi).
Axes of the slice: x: 4, y: 4, z: 16 (z_hi: 2, z_lo: 8; z = z_hi * 8 + z_lo), core: 2. Of those that a mesh axis runs over, the one named last changes fastest.
Arguments:
- tokens: bfloat16 [8, 16384, 768], P('dp', 'ctx'), may hold values from -40 to 40
- cotangent: bfloat16 [8, 16384, 768], P('dp', 'ctx'), may hold values from -200 to 200
- norm_gain: float32 [768], replicated, may hold values from 0.1 to 1.9
- conv_weight: bfloat16 [3, 768, 768], P(None, 'ctx'), may hold values from -0.125 to 0.125
- up_weight: bfloat16 [768, 1152], P('ctx'), may hold values from -0.21875 to 0.21875
- down_weight: bfloat16 [1152, 768], P('ctx'), may hold values from -0.1875 to 0.1875
- contig_first_bins: int32 [8], replicated, may hold values from 0 to 14847, as said below
Outputs:
- output: bfloat16 [8, 16384, 768], P('dp', 'ctx')
- input_grad: bfloat16 [8, 16384, 768], P('dp', 'ctx')
- down_grad: float32 [1152, 768], P('ctx', 'dp')
- gain_grad: float32 [768], P('dp')
The draws below stay inside these ranges and needn't reach their ends.
Inputs may be any that keep to these rules, and one draw needn't show every extreme that they name: contig_first_bins[0] = 0; the starts increase strictly, consecutive ones at least 1024 bins apart; the last contig starts at 14847.
All inputs are finite; a program needn't handle non-finite values.
Results may differ from the reference program's by a relative error of at most 0.0054.
Values may be sent and summed in bfloat16 or wider, within the bound.
A program may use at most 64 MiB of HBM per device.

```python
import math
import jax
import jax.numpy as jnp
from jax import lax

BLOCK_CHANNELS = 768
FF = 1152
DILATION_BINS = 64
BINS_DEV = 256
TOTAL = 16384
BATCH = 8
CONTIGS = 8


def draw_tokens(key, part):
    noise_key, row_key, chan_key = jax.random.split(key, 3)
    row_scale = jnp.exp(jax.random.uniform(row_key, (BATCH, TOTAL, 1), jnp.float32, math.log(0.3), math.log(3.0)))
    chan_scale = jnp.exp(jax.random.uniform(chan_key, (1, 1, BLOCK_CHANNELS), jnp.float32, math.log(0.3), math.log(3.0)))
    base = jax.random.truncated_normal(noise_key, -4.0, 4.0, (BATCH, TOTAL, BLOCK_CHANNELS), jnp.float32)
    return (base * row_scale * chan_scale).astype(jnp.bfloat16)


def draw_cotangent(key, part):
    noise_key = jax.random.fold_in(key, 0)
    heavy_key = jax.random.fold_in(key, 2)
    along = jnp.arange(TOTAL, dtype=jnp.float32)[None, :, None] / TOTAL
    segment_count = TOTAL // BINS_DEV
    chosen = jax.random.randint(heavy_key, (BATCH, 1), 0, segment_count, jnp.int32)
    segment_of_bin = jnp.arange(TOTAL, dtype=jnp.int32)[None, :] // BINS_DEV
    heavy = jnp.where(segment_of_bin == chosen, 5.0, 1.0).astype(jnp.float32)[:, :, None]
    base = jax.random.truncated_normal(noise_key, -4.0, 4.0, (BATCH, TOTAL, BLOCK_CHANNELS), jnp.float32)
    rising = 1.0 + 2.0 * along
    return (base * rising * heavy).astype(jnp.bfloat16)


def draw_contig_first_bins(key, part):
    spacing = TOTAL // CONTIGS
    jitter = jax.random.randint(key, (CONTIGS,), -2 * BINS_DEV, 2 * BINS_DEV, jnp.int32)
    counter = jnp.arange(CONTIGS, dtype=jnp.int32)
    starts = counter * spacing + jitter
    last_start = TOTAL - 6 * BINS_DEV - 1
    starts = jnp.where(counter == CONTIGS - 1, last_start, starts)
    return jnp.where(counter == 0, 0, starts).astype(jnp.int32)


def block_scale(own_key, shape, shards, least, largest):
    factor_of, own = 1.0, jax.random.fold_in(own_key, 6)
    for axis_at, blocks in shards:
        heights = jnp.exp(jax.random.uniform(jax.random.fold_in(own, axis_at), (blocks,), jnp.float32, least / len(shards), largest / len(shards)))
        factor_of = factor_of * jnp.repeat(heights, shape[axis_at] // blocks).reshape([-1 if axis == axis_at else 1 for axis in range(len(shape))])
    return factor_of


def gaussian(rng, dims, spread, most, pieces=(), held_as=jnp.bfloat16):
    array = spread * jax.random.normal(rng, dims, jnp.float32)
    if pieces:
        array = array * block_scale(rng, dims, pieces, -0.22, 0.18)
    return jnp.clip(array, -most, most).astype(held_as)


def setup_inputs(seed: int = 0) -> dict:
    arg_keys = jax.random.split(jax.random.key(seed), 8)
    tokens = draw_tokens(jax.random.fold_in(arg_keys[7], 71), 0)
    cotangent = draw_cotangent(jax.random.fold_in(arg_keys[7], 71), 0)
    norm_gain = jnp.clip(1.0 + 0.18 * jax.random.normal(arg_keys[2], (BLOCK_CHANNELS,), jnp.float32), 0.1, 1.9)
    conv_weight = gaussian(arg_keys[3], (3, BLOCK_CHANNELS, BLOCK_CHANNELS), (3 * BLOCK_CHANNELS) ** -0.5, 0.125, ((1, 64),))
    up_weight = gaussian(arg_keys[4], (BLOCK_CHANNELS, FF), BLOCK_CHANNELS ** -0.5, 0.21875, ((0, 64),))
    down_weight = gaussian(arg_keys[5], (FF, BLOCK_CHANNELS), FF ** -0.5, 0.1875, ((0, 64),))
    contig_first_bins = draw_contig_first_bins(jax.random.fold_in(arg_keys[7], 71), 0)
    return {"tokens": tokens, "cotangent": cotangent, "norm_gain": norm_gain, "conv_weight": conv_weight, "up_weight": up_weight, "down_weight": down_weight, "contig_first_bins": contig_first_bins}


root_half = 0.7071067811865476
inv_root_two_pi = 0.3989422804014327

def segment_lookup(bin_position, contig_first_bins):
    return lax.optimization_barrier(jnp.sum((contig_first_bins[None, :] <= bin_position[:, None]).astype(jnp.int32), axis=1))

def tap_masks(bin_position, contig_first_bins, overall_bin_count):
    current_segment = segment_lookup(bin_position, contig_first_bins)
    preceding_segment = segment_lookup(bin_position - DILATION_BINS, contig_first_bins)
    following_segment = segment_lookup(bin_position + DILATION_BINS, contig_first_bins)
    left_valid_mask = jnp.logical_and(bin_position >= DILATION_BINS, preceding_segment == current_segment)
    right_valid_mask = jnp.logical_and(bin_position + DILATION_BINS < overall_bin_count, following_segment == current_segment)
    return (left_valid_mask.astype(jnp.bfloat16)[:, None], right_valid_mask.astype(jnp.bfloat16)[:, None])

def gelu_value(pre_value):
    return 0.5 * pre_value * (1.0 + lax.erf(pre_value * root_half))

def gelu_slope(pre_value):
    return 0.5 * (1.0 + lax.erf(pre_value * root_half)) + pre_value * jnp.exp(-0.5 * pre_value * pre_value) * inv_root_two_pi

def one_sequence(tokens, cotangent, norm_gain, conv_weight, up_weight, down_weight, left_valid_mask, right_valid_mask):
    tok_float = tokens.astype(jnp.float32)
    inverse = lax.rsqrt(lax.optimization_barrier(jnp.mean(tok_float * tok_float, axis=1, keepdims=True)) + 1e-05)
    scaled = tok_float * inverse
    normalized_input = (scaled * norm_gain).astype(jnp.bfloat16)
    empty_padding_rows = jnp.zeros((DILATION_BINS, BLOCK_CHANNELS), jnp.bfloat16)
    preceding_value = jnp.concatenate([empty_padding_rows, normalized_input[:-DILATION_BINS]], axis=0) * left_valid_mask
    following_tap = jnp.concatenate([normalized_input[DILATION_BINS:], empty_padding_rows], axis=0) * right_valid_mask
    stacked = jnp.concatenate([preceding_value, normalized_input, following_tap], axis=1)
    conv_out = jnp.dot(stacked, conv_weight.reshape(3 * BLOCK_CHANNELS, BLOCK_CHANNELS), preferred_element_type=jnp.float32)
    mixed_sum = tok_float + conv_out
    pre_act = jnp.dot(mixed_sum.astype(jnp.bfloat16), up_weight, preferred_element_type=jnp.float32)
    hidden = gelu_value(pre_act).astype(jnp.bfloat16)
    output = (mixed_sum + jnp.dot(hidden, down_weight, preferred_element_type=jnp.float32)).astype(jnp.bfloat16)
    hidden_grad = jnp.dot(cotangent, down_weight.T, preferred_element_type=jnp.float32)
    pre_grad = (hidden_grad * gelu_slope(pre_act)).astype(jnp.bfloat16)
    mixed_grad = cotangent.astype(jnp.float32) + jnp.dot(pre_grad, up_weight.T, preferred_element_type=jnp.float32)
    convolution_gradient = mixed_grad.astype(jnp.bfloat16)
    following_gradient = jnp.concatenate([convolution_gradient[DILATION_BINS:], empty_padding_rows], axis=0) * right_valid_mask
    preceding_gradient = jnp.concatenate([empty_padding_rows, convolution_gradient[:-DILATION_BINS]], axis=0) * left_valid_mask
    back_stack = jnp.concatenate([following_gradient, convolution_gradient, preceding_gradient], axis=1)
    back_weight = jnp.transpose(conv_weight, (0, 2, 1)).reshape(3 * BLOCK_CHANNELS, BLOCK_CHANNELS)
    normed_grad = jnp.dot(back_stack, back_weight, preferred_element_type=jnp.float32)
    scaled_grad = normed_grad * norm_gain
    inner_mean = lax.optimization_barrier(jnp.mean(scaled_grad * scaled, axis=1, keepdims=True))
    input_grad = (mixed_grad + inverse * (scaled_grad - scaled * inner_mean)).astype(jnp.bfloat16)
    gain_term = lax.optimization_barrier(jnp.sum(normed_grad * scaled, axis=0))
    down_term = jnp.dot(hidden.T, cotangent, preferred_element_type=jnp.float32)
    return (output, input_grad, gain_term, down_term)

def reference(tokens, cotangent, norm_gain, conv_weight, up_weight, down_weight, contig_first_bins):
    bin_position = jnp.arange(TOTAL, dtype=jnp.int32)
    left_valid_mask, right_valid_mask = tap_masks(bin_position, contig_first_bins, TOTAL)

    def per_row(row_pair):
        return one_sequence(row_pair[0], row_pair[1], norm_gain, conv_weight, up_weight, down_weight, left_valid_mask, right_valid_mask)
    outputs, input_grads, gain_terms, down_terms = lax.map(per_row, (tokens, cotangent))
    factor = float(BATCH * TOTAL) ** (-0.5)
    down_grad = lax.optimization_barrier(jnp.sum(down_terms, axis=0)) * factor
    gain_grad = lax.optimization_barrier(jnp.sum(gain_terms, axis=0)) * factor
    return (outputs, input_grads, down_grad, gain_grad)
```

```python
import jax
import jax.numpy as jnp
from jax import lax
from jax.experimental import pallas as pl
from jax.experimental.pallas import tpu as pltpu
from jax.sharding import PartitionSpec as P

MESH = pl.DeviceIdType.MESH
root_half = 0.7071067811865476
inv_root_two_pi = 0.3989422804014327
factor = float(8 * 16384) ** (-0.5)


def place():
    ctx, dp = lax.axis_index("ctx"), lax.axis_index("dp")
    return ctx // 8, (ctx // 2) % 4, ctx % 2, dp // 2, dp % 2


def device(x, core, y, z):
    z = (z + 32) % 16
    return {"ctx": (z % 8) * 8 + ((x + 8) % 4) * 2 + core, "dp": ((y + 8) % 4) * 2 + z // 8}


def gather_kernel(conv, up, down, tok, full, halo, conv_shards, up_shards, down_shards, block, near_send, near_recv, far_send, far_recv, own_sem,
                  ring_send, ring_recv, pair_send, pair_recv, halo_send, halo_recv):
    zlo, x, core, y, zhi = place()
    z = zhi * 8 + zlo
    slot = x * 2 + core

    def remote(s, d, ss, rs, dev):
        return pltpu.make_async_remote_copy(src_ref=s, dst_ref=d, send_sem=ss, recv_sem=rs, device_id=dev,
                                            device_id_type=MESH)

    barrier = pltpu.get_barrier_semaphore()

    def greet(dev):
        pl.semaphore_signal(barrier, inc=1, device_id=dev, device_id_type=MESH)

    for j in range(1, 4):
        greet(device(x + j, core, y, z))
    for j in range(-1, 2, 2):
        greet(device(x, core, y + j, z))
    greet(device(x, 1 - core, y, z))
    for j in range(1, 5):
        for c in range(2):
            greet(device(x, c, y, z + j))
            greet(device(x, c, y, z - j))
    ctx, after = lax.axis_index("ctx"), {"dp": lax.axis_index("dp")}
    has_left, has_right = jnp.minimum(ctx, 1), jnp.minimum(63 - ctx, 1)
    left_device, right_device = {"ctx": ctx - has_left, **after}, {"ctx": ctx + has_right, **after}

    @pl.when(ctx > 0)
    def _():
        greet(left_device)

    @pl.when(ctx < 63)
    def _():
        greet(right_device)

    pl.semaphore_wait(barrier, 22 + has_left + has_right)

    to_left = remote(tok.at[0:64], halo.at[1], halo_send.at[0], halo_recv.at[1], left_device)
    to_right = remote(tok.at[192:256], halo.at[0], halo_send.at[1], halo_recv.at[0], right_device)
    spare_left = pltpu.make_async_copy(tok.at[0:64], halo.at[0], halo_recv.at[0])
    spare_right = pltpu.make_async_copy(tok.at[192:256], halo.at[1], halo_recv.at[1])

    @pl.when(ctx > 0)
    def _():
        to_left.start()

    @pl.when(ctx < 63)
    def _():
        to_right.start()

    @pl.when(ctx == 0)
    def _():
        spare_left.start()

    @pl.when(ctx == 63)
    def _():
        spare_right.start()

    partner = device(x, 1 - core, y, z)

    def share(mine, shards):
        cx = [remote(mine, shards.at[slot], near_send.at[j], near_recv.at[j], device(x + j, core, y, z)) for j in range(1, 4)]
        for c in cx:
            c.start()
        c0 = remote(mine, shards.at[slot], near_send.at[0], near_recv.at[0], partner)
        c0.start()
        keep = pltpu.make_async_copy(mine, shards.at[slot], own_sem.at[0])
        keep.start()
        fw = []
        for j in range(1, 4):
            cx[j - 1].wait_recv()
            r = shards.at[((x + 4 - j) % 4) * 2 + core]
            f = remote(r, r, near_send.at[3 + j], near_recv.at[3 + j], partner)
            f.start()
            fw.append(f)
        keep.wait()
        c0.wait_recv()
        for f in fw:
            f.wait_recv()
        for c in cx + [c0] + fw:
            c.wait_send()

    @pl.when(y < 2)
    def _():
        share(conv.at[pl.ds(y, 2)], conv_shards)

    @pl.when(y == 2)
    def _():
        share(up, up_shards)

    @pl.when(y == 3)
    def _():
        share(down, down_shards)

    @pl.when(y == 0)
    def _():
        parts = [conv_shards[i, 0] for i in range(8)] + [conv_shards[i, 1] for i in range(4)]
        block[...] = jnp.concatenate(parts, axis=0).reshape(2, 72, 768)

    @pl.when(y == 1)
    def _():
        parts = [conv_shards[i, 0] for i in range(4, 8)] + [conv_shards[i, 1] for i in range(8)]
        block[...] = jnp.concatenate(parts, axis=0).reshape(2, 72, 768)

    @pl.when(y == 2)
    def _():
        tails = [jnp.concatenate([up_shards[i, :, 768:1152] for i in r], axis=0) for r in (range(4), range(4, 8))]
        top = jnp.concatenate([up_shards[i, :, 0:768] for i in range(8)], axis=0)
        block[...] = jnp.concatenate([top, jnp.concatenate(tails, axis=1)], axis=0).reshape(2, 72, 768)

    @pl.when(y == 3)
    def _():
        block[...] = jnp.concatenate([down_shards[i] for i in range(8)], axis=0).reshape(2, 72, 768)

    def cols(m):
        return pl.ds(pl.multiple_of((m % 2) * 384, 384), 384)

    keeper = zlo // 4
    rect = block.at[x // 2, :, cols(x)]
    target = full.at[zlo, y, x // 2, :, cols(x)]

    for sign, c in ((1, 0), (-1, 1)):
        @pl.when(core == c)
        def _():
            for j in range(1, 5 if sign == 1 else 4):
                remote(rect, target, far_send.at[j - 1], far_recv.at[zlo % 4], device(x, keeper, y, z + sign * j)).start()

    @pl.when(core == keeper)
    def _():
        own = pltpu.make_async_copy(rect, target, own_sem.at[1])
        own.start()
        own.wait()

    base = core * 4

    def block_of(i):
        return base + (zlo + i) % 4

    def far_wait(i, carry):
        zb = block_of(i)

        @pl.when(zb != zlo)
        def _():
            t = full.at[zb, y, x // 2, :, cols(x)]
            remote(t, t, far_send.at[0], far_recv.at[zb % 4], partner).wait_recv()
        return carry

    def xpart(zb, m):
        m = (m + 8) % 4
        return full.at[zb, y, m // 2, :, cols(m)]

    def ypart(zb, m):
        return full.at[zb, (m + 8) % 4, x // 2, :, cols(x)]

    def yslab(zb, m):
        return full.at[zb, (m + 8) % 4]

    def xslab(zb, m):
        m = (m + 8) % 4
        return full.at[zb, :, m // 2, :, cols(m)]

    def ring(stage, part, me, peer, before, after):
        def start(i, carry):
            before(i)
            r = part(block_of(i), me)
            remote(r, r, ring_send.at[stage, 0, i], ring_recv.at[stage, 0, i], peer(1)).start()
            remote(r, r, ring_send.at[stage, 1, i], ring_recv.at[stage, 1, i], peer(-1)).start()
            after(i, 0, me)
            return carry

        def forward(i, carry):
            zb = block_of(i)
            way = 1 - 2 * (i // 2)
            r = part(zb, me - 1)
            remote(r, r, ring_send.at[stage, 0, i], ring_recv.at[stage, 0, i], peer(1)).wait_recv()
            after(i, 1, me - 1)
            r = part(zb, me + 1)
            remote(r, r, ring_send.at[stage, 1, i], ring_recv.at[stage, 1, i], peer(-1)).wait_recv()
            after(i, 2, me + 1)
            r = part(zb, me - way)
            remote(r, r, ring_send.at[stage, 2, i], ring_recv.at[stage, 2, i], peer(way)).start()
            return carry

        def finish(i):
            r = part(block_of(i), me + 2)
            remote(r, r, ring_send.at[stage, 2, i], ring_recv.at[stage, 2, i], peer(1)).wait_recv()
            after(i, 3, me + 2)

        return start, forward, finish

    def drain(stage, part, me):
        def body(i, carry):
            r = part(block_of(i), me)
            for w in range(3):
                remote(r, r, ring_send.at[stage, w, i], ring_recv.at[stage, w, i], partner).wait_send()
            return carry
        lax.fori_loop(0, 4, body, 0)

    def whole(part1, me1, peer1, part2, me2, peer2):
        def nothing(i, n, m):
            return None

        def hand(i, n, m):
            r = part2(block_of(i), m)
            remote(r, r, pair_send.at[n, i], pair_recv.at[n, i], partner).start()

        start1, forward1, finish1 = ring(0, part1, me1, peer1, lambda i: far_wait(i, 0), nothing)
        start2, forward2, finish2 = ring(1, part2, me2, peer2, finish1, hand)
        lax.fori_loop(0, 4, start1, 0)
        lax.fori_loop(0, 4, forward1, 0)
        lax.fori_loop(0, 4, start2, 0)
        lax.fori_loop(0, 4, forward2, 0)

        def last(i, carry):
            finish2(i)
            return carry
        lax.fori_loop(0, 4, last, 0)
        drain(0, part1, me1)
        drain(1, part2, me2)

    def along_x(j):
        return device(x + j, core, y, z)

    def along_y(j):
        return device(x, core, y + j, z)

    def pair_wait(part_there, me_there, part_here, me_here):
        def body(i, carry):
            there = (1 - core) * 4 + (zlo + i) % 4
            for n, m in enumerate((0, -1, 1, 2)):
                r = part_there(there, me_there + m)
                remote(r, r, pair_send.at[n, i], pair_recv.at[n, i], partner).wait_recv()
                s = part_here(block_of(i), me_here + m)
                remote(s, s, pair_send.at[n, i], pair_recv.at[n, i], partner).wait_send()
            return carry
        lax.fori_loop(0, 4, body, 0)

    @pl.when(core == 0)
    def _():
        whole(xpart, x, along_x, yslab, y, along_y)
        pair_wait(xslab, x, yslab, y)

    @pl.when(core == 1)
    def _():
        whole(ypart, y, along_y, xslab, x, along_x)
        pair_wait(yslab, y, xslab, x)

    for sign, c in ((1, 0), (-1, 1)):
        @pl.when(core == c)
        def _():
            for j in range(1, 5 if sign == 1 else 4):
                remote(rect, target, far_send.at[j - 1], far_recv.at[zlo % 4], partner).wait_send()

    @pl.when(ctx > 0)
    def _():
        to_left.wait_send()
        to_right.wait_recv()

    @pl.when(ctx < 63)
    def _():
        to_right.wait_send()
        to_left.wait_recv()

    @pl.when(ctx == 0)
    def _():
        spare_left.wait()

    @pl.when(ctx == 63)
    def _():
        spare_right.wait()


def gather_weights(conv, up, down, tok):
    dma = pltpu.SemaphoreType.DMA
    vmem = pl.BlockSpec(memory_space=pltpu.VMEM)
    return pl.pallas_call(
        gather_kernel,
        out_shape=(
            jax.ShapeDtypeStruct((8, 4, 2, 72, 768), jnp.bfloat16),
            jax.ShapeDtypeStruct((2, 64, 768), jnp.bfloat16),
        ),
        in_specs=[vmem, vmem, vmem, pl.BlockSpec(memory_space=pl.ANY)],
        out_specs=(pl.BlockSpec(memory_space=pl.ANY), pl.BlockSpec(memory_space=pl.ANY)),
        scratch_shapes=[
            pltpu.VMEM((8, 2, 12, 768), jnp.bfloat16),
            pltpu.VMEM((8, 12, 1152), jnp.bfloat16),
            pltpu.VMEM((8, 18, 768), jnp.bfloat16),
            pltpu.VMEM((2, 72, 768), jnp.bfloat16),
            dma((7,)), dma((7,)), dma((4,)), dma((4,)), dma((2,)),
            dma((2, 3, 4)), dma((2, 3, 4)), dma((4, 4)), dma((4, 4)), dma((2,)), dma((2,)),
        ],
        compiler_params=pltpu.CompilerParams(collective_id=0, has_side_effects=True),
        name="gather_weights",
    )(conv, up, down, tok)


def turned(lhs, rhs):
    return lax.dot_general(lhs, rhs, (((1,), (1,)), ((), ())), preferred_element_type=jnp.float32)


def plain(lhs, rhs):
    return jnp.dot(lhs, rhs, preferred_element_type=jnp.float32)


def block_kernel(tok, cot, halo, gain, starts, w0, w1, w2, up_a, up_b, dn,
                 out, grad, down_part, gain_total,
                 wide, slope, hidden, mixed_keep, cot_half, cgrad, cgrad_halo,
                 share, pair_out, pair_in, ring_out, ring_in, next_out, next_in, far_out, far_in, last_out, last_in,
                 gain_mine, gain_pair, gain_x, gain_y, gain_z, gain_full,
                 pair_send, pair_recv, ring_send, ring_recv, next_send, next_recv, far_send, far_recv,
                 last_send, last_recv, halo_send, halo_recv, gain_send, gain_recv):
    zlo, x, core, y, zhi = place()
    z = zhi * 8 + zlo
    ctx, same = lax.axis_index("ctx"), {"dp": lax.axis_index("dp")}
    partner = device(x, 1 - core, y, z)
    has_left, has_right = jnp.minimum(ctx, 1), jnp.minimum(63 - ctx, 1)
    left_device, right_device = {"ctx": ctx - has_left, **same}, {"ctx": ctx + has_right, **same}
    ahead = x * (1 - core) + y * core
    across = y * (1 - core) + x * core
    piece = ahead * 4 + across
    far_z = piece // 2 + 8 * core

    def remote(s, d, ss, rs, dev):
        return pltpu.make_async_remote_copy(src_ref=s, dst_ref=d, send_sem=ss, recv_sem=rs, device_id=dev,
                                            device_id_type=MESH)

    def along_first(j):
        return device(x + j * (1 - core), core, y + j * core, z)

    def along_second(j):
        return device(x + j * core, core, y + j * (1 - core), z)

    barrier = pltpu.get_barrier_semaphore()

    def greet(dev):
        pl.semaphore_signal(barrier, inc=1, device_id=dev, device_id_type=MESH)

    def greet_far(j, carry):
        greet(device(x, core, y, z + j))
        return carry
    lax.fori_loop(1, 16, greet_far, 0)

    def greet_near(j, carry):
        greet(device(x + j // 8, (core + j) % 2, y + (j // 2) % 4, z))
        return carry
    lax.fori_loop(1, 32, greet_near, 0)

    @pl.when(ctx > 0)
    def _():
        greet(left_device)

    @pl.when(ctx < 63)
    def _():
        greet(right_device)

    bins = ctx * 256 + lax.broadcasted_iota(jnp.int32, (256, 1), 0)
    left_ok = bins >= 64
    right_ok = bins + 64 < 16384
    for c in range(8):
        first = starts[c]
        left_ok = jnp.logical_and(left_ok, jnp.logical_or(first <= bins - 64, first > bins))
        right_ok = jnp.logical_and(right_ok, jnp.logical_or(first <= bins, first > bins + 64))

    def norm(v):
        v = v.astype(jnp.float32)
        inverse = lax.rsqrt(jnp.mean(v * v, axis=1, keepdims=True) + 1e-05)
        return v * inverse, inverse

    wide[0:64] = (norm(halo[0])[0] * gain[...]).astype(jnp.bfloat16)
    wide[64:320] = (norm(tok[...])[0] * gain[...]).astype(jnp.bfloat16)
    wide[320:384] = (norm(halo[1])[0] * gain[...]).astype(jnp.bfloat16)

    for h in range(2):
        col = lax.broadcasted_iota(jnp.int32, (768, 384), 1)
        row = lax.broadcasted_iota(jnp.int32, (768, 384), 0)
        ys = (col >= 96).astype(jnp.int32) + (col >= 192).astype(jnp.int32) + (col >= 288).astype(jnp.int32)
        pick = jnp.where(row == col + 96 * ys + 96 * h, 1.0, 0.0).astype(jnp.bfloat16)
        cot_half[h] = plain(cot[...], pick).astype(jnp.bfloat16)

    def masked(ok, v):
        return jnp.where(ok, v.astype(jnp.float32), 0.0).astype(jnp.bfloat16)

    taps = [r[...].reshape(768, 768) for r in (w0, w1, w2)]
    acc = plain(masked(left_ok, wide[0:256]), taps[0]) + plain(wide[64:320], taps[1])
    acc = acc + plain(masked(right_ok, wide[128:384]), taps[2])
    mixed = tok[...].astype(jnp.float32) + acc
    mixed_keep[...] = mixed
    low = mixed.astype(jnp.bfloat16)
    for f in range(3):
        if f < 2:
            w = up_a[:, :, f * 384:(f + 1) * 384].reshape(768, 384)
        else:
            w = jnp.concatenate([up_b[:, :, 0:384], up_b[:, :, 384:768]], axis=1).reshape(768, 384)
        pre = plain(low, w)
        bend = 0.5 * (1.0 + lax.erf(pre * root_half))
        at = slice(f * 384, (f + 1) * 384)
        hidden[:, at] = (pre * bend).astype(jnp.bfloat16)
        slope[:, at] = bend + pre * jnp.exp(-0.5 * pre * pre) * inv_root_two_pi

    def weight_grad(h):
        g = lax.dot_general(hidden[...], cot_half[h], (((0,), (0,)), ((), ())), preferred_element_type=jnp.float32)
        return g.reshape(16, 72, 384)

    pair_out[...] = weight_grad(1 - core).astype(jnp.bfloat16)
    pl.semaphore_wait(barrier, 46 + has_left + has_right)
    pair = remote(pair_out, pair_in, pair_send.at[0], pair_recv.at[0], partner)
    pair.start()
    share[...] = weight_grad(core)
    down = dn[...].reshape(1152, 768)
    pre_grad = (turned(cot[...], down) * slope[...]).astype(jnp.bfloat16)
    pair.wait_recv()
    share[...] = share[...] + pair_in[...].astype(jnp.float32)
    ring_out[...] = share[...].astype(jnp.bfloat16)
    ring = [remote(ring_out.at[pl.ds(((ahead + j) % 4) * 4, 4)], ring_in.at[j - 1], ring_send.at[j - 1],
                   ring_recv.at[j - 1], along_first(j)) for j in range(1, 4)]
    for c in ring:
        c.start()

    mixed_grad = cot[...].astype(jnp.float32)
    mixed_grad = mixed_grad + turned(pre_grad[:, 0:768], up_a[...].reshape(768, 768))
    w = jnp.concatenate([up_b[:, :, 0:384], up_b[:, :, 384:768]], axis=1).reshape(768, 384)
    mixed_grad = mixed_grad + turned(pre_grad[:, 768:1152], w)
    slope[:, 0:768] = mixed_grad
    cgrad[...] = mixed_grad.astype(jnp.bfloat16)
    to_left = remote(cgrad.at[0:64], cgrad_halo.at[1], halo_send.at[0], halo_recv.at[1], left_device)
    to_right = remote(cgrad.at[192:256], cgrad_halo.at[0], halo_send.at[1], halo_recv.at[0], right_device)

    @pl.when(ctx > 0)
    def _():
        to_left.start()

    @pl.when(ctx < 63)
    def _():
        to_right.start()

    out[...] = (mixed_keep[...] + plain(hidden[...], down)).astype(jnp.bfloat16)

    for c in ring:
        c.wait_recv()
    mine = share[pl.ds(ahead * 4, 4)]
    for j in range(3):
        mine = mine + ring_in[j].astype(jnp.float32)
    share[0:4] = mine
    next_out[...] = mine.astype(jnp.bfloat16)
    second = [remote(next_out.at[(across + j) % 4], next_in.at[j - 1], next_send.at[j - 1], next_recv.at[j - 1],
                     along_second(j)) for j in range(1, 4)]
    for c in second:
        c.start()

    @pl.when(ctx > 0)
    def _():
        to_left.wait_send()
        to_right.wait_recv()

    @pl.when(ctx < 63)
    def _():
        to_right.wait_send()
        to_left.wait_recv()

    @pl.when(ctx == 0)
    def _():
        cgrad_halo[0] = jnp.zeros((64, 768), jnp.bfloat16)

    @pl.when(ctx == 63)
    def _():
        cgrad_halo[1] = jnp.zeros((64, 768), jnp.bfloat16)

    wide[0:64] = cgrad_halo[0]
    wide[64:320] = cgrad[...]
    wide[320:384] = cgrad_halo[1]
    normed_grad = turned(masked(right_ok, wide[128:384]), taps[0]) + turned(wide[64:320], taps[1])
    normed_grad = normed_grad + turned(masked(left_ok, wide[0:256]), taps[2])
    scaled, inverse = norm(tok[...])
    gain_term = jnp.sum(normed_grad * scaled, axis=0, keepdims=True)
    for h in range(2):
        gain_mine[h] = gain_term[:, h * 384:(h + 1) * 384]
    g_pair = remote(gain_mine.at[1 - core], gain_pair, gain_send.at[0], gain_recv.at[0], partner)
    g_pair.start()
    scaled_grad = normed_grad * gain[...]
    inner = jnp.mean(scaled_grad * scaled, axis=1, keepdims=True)
    grad[...] = (slope[:, 0:768] + inverse * (scaled_grad - scaled * inner)).astype(jnp.bfloat16)

    for c in second:
        c.wait_recv()
    total = share[across]
    for j in range(3):
        total = total + next_in[j].astype(jnp.float32)
    share[4] = total
    far_out[...] = total.astype(jnp.bfloat16)
    far = remote(far_out, far_in.at[z], far_send.at[0], far_recv.at[z], device(x, core, y, far_z))

    @pl.when(z != far_z)
    def _():
        far.start()

    g_pair.wait_recv()
    gain_x[ahead] = gain_mine[core] + gain_pair[...]
    hops = [remote(gain_x.at[ahead], gain_x.at[ahead], gain_send.at[j], gain_recv.at[j], along_first(j)) for j in range(1, 4)]
    for c in hops:
        c.start()
    for c in hops:
        c.wait()
    gain_y[across] = (gain_x[0] + gain_x[1]) + (gain_x[2] + gain_x[3])
    hops = [remote(gain_y.at[across], gain_y.at[across], gain_send.at[3 + j], gain_recv.at[3 + j], along_second(j))
            for j in range(1, 4)]
    for c in hops:
        c.start()
    for c in hops:
        c.wait()
    gain_z[z] = (gain_y[0] + gain_y[1]) + (gain_y[2] + gain_y[3])

    def spread(j, carry):
        remote(gain_z.at[z], gain_z.at[z], gain_send.at[6 + j], gain_recv.at[6 + j], device(x, core, y, z + j)).start()
        return carry
    lax.fori_loop(1, 16, spread, 0)

    @pl.when(z == far_z)
    def _():
        def take(j, carry):
            zz = (z + j) % 16
            remote(far_out, far_in.at[zz], far_send.at[0], far_recv.at[zz], partner).wait_recv()
            share[4] = share[4] + far_in[zz].astype(jnp.float32)
            return carry
        lax.fori_loop(1, 16, take, 0)
        for i in range(4):
            for b in range(4):
                last_out[i * 4 + b] = jnp.zeros((24, 128), jnp.float32)
                last_out[i * 4 + b, 0:18, 0:96] = share[4, 18 * i:18 * i + 18, 96 * b:96 * b + 96]

        def hand(n, carry):
            i, b = n // 4, n % 4
            tx, tc = (piece % 2) * 2 + i // 2, i % 2
            myself = jnp.logical_and(jnp.logical_and(tx == x, tc == core), b == y)

            @pl.when(jnp.logical_not(myself))
            def _():
                remote(last_out.at[n], last_in, last_send.at[n], last_recv.at[0], device(tx, tc, b, z)).start()

            @pl.when(myself)
            def _():
                last_in[...] = last_out[n]
            return carry
        lax.fori_loop(0, 16, hand, 0)

        def handed(n, carry):
            i, b = n // 4, n % 4
            tx, tc = (piece % 2) * 2 + i // 2, i % 2
            myself = jnp.logical_and(jnp.logical_and(tx == x, tc == core), b == y)

            @pl.when(jnp.logical_not(myself))
            def _():
                remote(last_out.at[n], last_in, last_send.at[n], last_recv.at[0], partner).wait_send()
            return carry
        lax.fori_loop(0, 16, handed, 0)

    def arrive(j, carry):
        remote(gain_z.at[z], gain_z.at[z], gain_send.at[6 + j], gain_recv.at[6 + j], partner).wait()
        return carry
    lax.fori_loop(1, 16, arrive, 0)
    whole = gain_z[0]
    for n in range(1, 16):
        whole = whole + gain_z[n]
    gain_full[core] = whole
    g_last = remote(gain_full.at[core], gain_full.at[core], gain_send.at[22], gain_recv.at[22], partner)
    g_last.start()

    source = zlo * 2 + x // 2
    source_x = (source // 4) * (1 - zhi) + (source % 4) * zhi
    source_y = (source % 4) * (1 - zhi) + (source // 4) * zhi
    own_source = jnp.logical_and(jnp.logical_and(source_x == x, source_y == y), core == zhi)

    @pl.when(jnp.logical_not(own_source))
    def _():
        remote(last_out.at[0], last_in, last_send.at[0], last_recv.at[0], partner).wait_recv()

    down_part[...] = last_in[0:18, 0:96] * factor
    g_last.wait()
    for h in range(2):
        gain_total[:, h * 384:(h + 1) * 384] = gain_full[h] * factor

    @pl.when(z != far_z)
    def _():
        far.wait_send()
    g_pair.wait_send()
    pair.wait_send()
    for c in ring + second:
        c.wait_send()


def run_block(tok, cot, halo, gain, starts, full):
    f32, bf16 = jnp.float32, jnp.bfloat16
    dma = pltpu.SemaphoreType.DMA
    vmem = pl.BlockSpec(memory_space=pltpu.VMEM)

    def rows(count, at):
        return pl.BlockSpec((8, count, 768), lambda i: (0, at, 0), pipeline_mode=pl.Buffered(1))

    return pl.pallas_call(
        block_kernel,
        grid=(1,),
        out_shape=(
            jax.ShapeDtypeStruct((256, 768), bf16), jax.ShapeDtypeStruct((256, 768), bf16),
            jax.ShapeDtypeStruct((18, 96), f32), jax.ShapeDtypeStruct((1, 768), f32),
        ),
        in_specs=[vmem, vmem, vmem, vmem, pl.BlockSpec(memory_space=pltpu.SMEM),
                  rows(96, 0), rows(96, 1), rows(96, 2), rows(96, 3), rows(48, 8), rows(144, 3)],
        out_specs=(vmem, vmem, vmem, vmem),
        scratch_shapes=[
            pltpu.VMEM((384, 768), bf16), pltpu.VMEM((256, 1152), f32), pltpu.VMEM((256, 1152), bf16),
            pltpu.VMEM((256, 768), f32), pltpu.VMEM((2, 256, 384), bf16), pltpu.VMEM((256, 768), bf16),
            pltpu.VMEM((2, 64, 768), bf16),
            pltpu.VMEM((16, 72, 384), f32), pltpu.VMEM((16, 72, 384), bf16), pltpu.VMEM((16, 72, 384), bf16),
            pltpu.VMEM((16, 72, 384), bf16), pltpu.VMEM((3, 4, 72, 384), bf16),
            pltpu.VMEM((4, 72, 384), bf16), pltpu.VMEM((3, 72, 384), bf16),
            pltpu.VMEM((72, 384), bf16), pltpu.VMEM((16, 72, 384), bf16),
            pltpu.VMEM((16, 24, 128), f32), pltpu.VMEM((24, 128), f32),
            pltpu.VMEM((2, 1, 384), f32), pltpu.VMEM((1, 384), f32), pltpu.VMEM((4, 1, 384), f32),
            pltpu.VMEM((4, 1, 384), f32), pltpu.VMEM((16, 1, 384), f32), pltpu.VMEM((2, 1, 384), f32),
            dma((1,)), dma((1,)), dma((3,)), dma((3,)), dma((3,)), dma((3,)), dma((1,)), dma((16,)),
            dma((16,)), dma((1,)), dma((2,)), dma((2,)), dma((23,)), dma((23,)),
        ],
        compiler_params=pltpu.CompilerParams(collective_id=1, has_side_effects=True, vmem_limit_bytes=60000 * 1024),
        name="block",
    )(tok, cot, halo, gain, starts, full, full, full, full, full, full)


def body(tokens, cotangent, norm_gain, conv_weight, up_weight, down_weight, contig_first_bins):
    tok, cot = tokens.reshape(256, 768), cotangent.reshape(256, 768)
    full, halo = gather_weights(conv_weight, up_weight, down_weight, tok)
    output, input_grad, down_part, gain_total = run_block(
        tok, cot, halo, norm_gain.reshape(1, 768), contig_first_bins, full.reshape(8, 576, 768))
    gain_part = lax.dynamic_slice_in_dim(gain_total[0], lax.axis_index("dp") * 96, 96)
    return output.reshape(tokens.shape), input_grad.reshape(tokens.shape), down_part, gain_part


def solution(mesh):
    placed = (
        P("dp", "ctx", None),
        P("dp", "ctx", None),
        P(),
        P(None, "ctx", None),
        P("ctx", None),
        P("ctx", None),
        P(),
    )
    return jax.shard_map(
        body,
        mesh=mesh,
        in_specs=placed,
        out_specs=(P("dp", "ctx", None), P("dp", "ctx", None), P("ctx", "dp"), P("dp")),
        check_vma=False,
    )
```
